32 devices in a mesh: az: 8 (over y, x, core), rg: 4 (over z).
Axes of the slice: x: 2, y: 2, z: 4, core: 2. Of those that a mesh axis runs over, the one named last changes fastest.
Arguments:
- reference_slc: bfloat16 [2, 768, 12288], P(None, 'az', 'rg'), may hold values from -6 to 6
- secondary_slc: bfloat16 [2, 768, 12288], P(None, 'az', 'rg'), may hold values from -6 to 6
- chip_offsets: int32 [2, 8, 384], P(None, 'az', 'rg'), may hold values from -80 to 80, as said below
- src_row: int32 [768], replicated, may hold values from 0 to 767, as said below
- line_owner: int32 [768], replicated, may hold values from 0 to 31, as said below
- band_start: int32 [12288], replicated, may hold values from -64 to 12343, as said below
- band_taps: bfloat16 [8, 12288], replicated, may hold values from -2.09375 to 2.09375
Outputs:
- est_offsets: float32 [2, 8, 384], P(None, 'az', 'rg')
- resampled: bfloat16 [2, 1024, 12288], P(None, ('az', 'rg'))
The draws below stay inside these ranges and needn't reach their ends.
Inputs may be any that keep to these rules, and one draw needn't show every extreme that they name: chip_offsets[0] lies within -80 and 80, chip_offsets[1] within -48 and 48. `src_row`: the source row of line i lies within 8 rows of i. `line_owner`: for every owner and every azimuth tile, at most 4 lines of that owner take their source rows from that tile, and an owner holds at most 32 lines; both bounds are met in every draw. band_start[j] lies within j - 64 and j + 56.
All inputs are finite; a program needn't handle non-finite values.
Results may differ from the reference program's by a relative error of at most 0.008.
Values may be sent and summed in bfloat16 or wider, within the bound.
A program may use at most 128 MiB of HBM per device.

```python
import math
import jax
import jax.numpy as jnp
from jax import lax

CHIP_LEN = 64
OVERSAMPLE = 16
LAG_COUNT = 48
TAP_COUNT = 8
SPACING = 32
MARGIN = 64
MAX_SHIFT = 8
LINES_DEV = 96
TILES_AZ = 8
ALL_LINES = 768
ALL_COLUMNS = 12288
CHIPS_ALL = 384
REF_RIM = 16
AZ_REACH = 80
RG_REACH = 48
OWNERS = 32
BUSY_OWNERS = 4
CALM_OWNERS = 28
PAIR_CAP = 4
OWNER_CAP = 32


def plan_lines(key):
    base = jax.random.fold_in(key, 71)
    shift_key = jax.random.fold_in(base, 1)
    order_key = jax.random.fold_in(base, 2)
    turn_key = jax.random.fold_in(base, 3)
    line_ids = jnp.arange(ALL_LINES, dtype=jnp.int32)
    line_moves = jax.random.randint(shift_key, (ALL_LINES,), -MAX_SHIFT, MAX_SHIFT + 1)
    line_moves = line_moves.at[0].set(-MAX_SHIFT).at[ALL_LINES - 1].set(MAX_SHIFT)
    source = jnp.clip(line_ids + line_moves, 0, ALL_LINES - 1)
    tile_of = source // LINES_DEV
    tile_hot = (tile_of[:, None] == jnp.arange(TILES_AZ, dtype=jnp.int32)[None, :]).astype(jnp.int32)
    tile_rank = jnp.sum(jnp.cumsum(tile_hot, axis=0) * tile_hot, axis=1) - 1
    shuffled = jax.random.permutation(order_key, OWNERS)
    heavy_set = shuffled[:BUSY_OWNERS]
    light_set = shuffled[BUSY_OWNERS:]
    light_turn = jax.random.randint(turn_key, (TILES_AZ,), 0, CALM_OWNERS)
    heavy_pick = heavy_set[jnp.minimum(tile_rank // PAIR_CAP, BUSY_OWNERS - 1)]
    light_pick = light_set[(tile_rank - PAIR_CAP * BUSY_OWNERS + light_turn[tile_of]) % CALM_OWNERS]
    owners = jnp.where(tile_rank < PAIR_CAP * BUSY_OWNERS, heavy_pick, light_pick)
    return (source.astype(jnp.int32), owners.astype(jnp.int32))


def draw_src_row(key, part):
    return plan_lines(key)[0]


def draw_line_owner(key, part):
    return plan_lines(key)[1]


def draw_chip_offsets(key, part):
    az_key = jax.random.fold_in(key, 5)
    rg_key = jax.random.fold_in(key, 6)
    az_part = jax.random.randint(az_key, (TILES_AZ, CHIPS_ALL), -AZ_REACH, AZ_REACH + 1)
    az_part = az_part.at[0, 0].set(-AZ_REACH).at[TILES_AZ - 1, CHIPS_ALL - 1].set(AZ_REACH)
    rg_part = jax.random.randint(rg_key, (TILES_AZ, CHIPS_ALL), -RG_REACH, RG_REACH + 1)
    rg_part = rg_part.at[0, 1].set(-RG_REACH).at[TILES_AZ - 1, 0].set(RG_REACH)
    return jnp.stack([az_part, rg_part]).astype(jnp.int32)


def draw_band_start(key, part):
    jitter = jax.random.randint(jax.random.fold_in(key, 9), (ALL_COLUMNS,), -MARGIN, MARGIN - TAP_COUNT + 1)
    jitter = jitter.at[0].set(-MARGIN).at[ALL_COLUMNS - 1].set(MARGIN - TAP_COUNT)
    return (jnp.arange(ALL_COLUMNS, dtype=jnp.int32) + jitter).astype(jnp.int32)


def levels(rng, shape, shards, smallest, top_value):
    def one(axis_at, parts):
        steps = jax.random.uniform(jax.random.fold_in(jax.random.fold_in(rng, 6), axis_at), (parts,), jnp.float32, smallest / len(shards), top_value / len(shards))
        return jnp.repeat(jnp.exp(steps), shape[axis_at] // parts).reshape((-1,) + (1,) * (len(shape) - axis_at - 1))

    gain = one(*shards[0])
    for cut in shards[1:]:
        gain = gain * one(*cut)
    return gain


def centred(own_key, shape, spread, bound, shards=(), held_as=jnp.bfloat16):
    result = spread * jax.random.normal(own_key, shape, jnp.float32)
    if shards:
        result = result * levels(own_key, shape, shards, -0.22, 0.18)
    return jnp.clip(result, -bound, bound).astype(held_as)


def setup_inputs(seed: int = 0) -> dict:
    arg_keys = jax.random.split(jax.random.key(seed), 8)
    return {
        "reference_slc": centred(arg_keys[0], (2, ALL_LINES, ALL_COLUMNS), 1.0, 6.0, ((1, 8), (2, 4))),
        "secondary_slc": centred(arg_keys[1], (2, ALL_LINES, ALL_COLUMNS), 1.0, 6.0, ((1, 8), (2, 4))),
        "chip_offsets": draw_chip_offsets(jax.random.fold_in(arg_keys[7], 71), 0),
        "src_row": draw_src_row(jax.random.fold_in(arg_keys[7], 71), 0),
        "line_owner": draw_line_owner(jax.random.fold_in(arg_keys[7], 71), 0),
        "band_start": draw_band_start(jax.random.fold_in(arg_keys[7], 71), 0),
        "band_taps": centred(arg_keys[6], (TAP_COUNT, ALL_COLUMNS), 0.35, 2.09375),
    }


PHASE_RATE = 2.0
EPS = 1e-06

def make_tables():
    indices = jnp.arange(CHIP_LEN, dtype=jnp.int32)
    product = indices[:, None] * indices[None, :] % CHIP_LEN
    angles = -2.0 * math.pi / CHIP_LEN * product.astype(jnp.float32)
    scaling = 1.0 / math.sqrt(CHIP_LEN)
    four_re = (jnp.cos(angles) * scaling).astype(jnp.bfloat16)
    four_im = (jnp.sin(angles) * scaling).astype(jnp.bfloat16)
    lag_steps = jnp.arange(LAG_COUNT, dtype=jnp.int32) - LAG_COUNT // 2
    frequency = jnp.where(indices < CHIP_LEN // 2, indices, indices - CHIP_LEN)
    phase_turns = lag_steps[:, None] * frequency[None, :] % (OVERSAMPLE * CHIP_LEN)
    lifted = 2.0 * math.pi / (OVERSAMPLE * CHIP_LEN) * phase_turns.astype(jnp.float32)
    lift_re = (jnp.cos(lifted) * scaling).astype(jnp.bfloat16)
    lift_im = (jnp.sin(lifted) * scaling).astype(jnp.bfloat16)
    lag_values = lag_steps.astype(jnp.float32) / OVERSAMPLE
    return (four_re, four_im, lift_re, lift_im, lag_values)

def rounded(values):
    return lax.optimization_barrier(values.astype(jnp.bfloat16)).astype(jnp.float32)

def spectrum(chip_re, chip_im, four_re, four_im):
    half_re = rounded(jnp.einsum('px,xgy->pgy', four_re, chip_re) - jnp.einsum('px,xgy->pgy', four_im, chip_im))
    half_im = rounded(jnp.einsum('px,xgy->pgy', four_re, chip_im) + jnp.einsum('px,xgy->pgy', four_im, chip_re))
    spec_re = jnp.einsum('pgy,qy->pgq', half_re, four_re) - jnp.einsum('pgy,qy->pgq', half_im, four_im)
    spec_im = jnp.einsum('pgy,qy->pgq', half_re, four_im) + jnp.einsum('pgy,qy->pgq', half_im, four_re)
    return (spec_re, spec_im)

def reference(reference_slc, secondary_slc, chip_offsets, src_row, line_owner, band_start, band_taps):
    four_re, four_im, lift_re, lift_im, lag_values = make_tables()
    four_re = four_re.astype(jnp.float32)
    four_im = four_im.astype(jnp.float32)
    lift_re = lift_re.astype(jnp.float32)
    lift_im = lift_im.astype(jnp.float32)
    sec_pad = jnp.pad(secondary_slc, ((0, 0), (MARGIN, MARGIN), (MARGIN, MARGIN)))
    first_row = LINES_DEV // 2 - CHIP_LEN // 2
    block_total = CHIPS_ALL + CHIP_LEN // SPACING - 1

    def per_tile(tile_index):
        row_first = (tile_index * LINES_DEV + first_row).astype(jnp.int32)
        ref_rows = lax.dynamic_slice(reference_slc, (jnp.int32(0), row_first, jnp.int32(0)), (2, CHIP_LEN, ALL_COLUMNS))
        offsets = lax.dynamic_index_in_dim(chip_offsets, tile_index, axis=1, keepdims=False)
        padded = jnp.pad(ref_rows, ((0, 0), (0, 0), (REF_RIM, REF_RIM)))
        blocks = padded.reshape(2, CHIP_LEN, block_total, SPACING)
        ref_chips = jnp.concatenate([blocks[:, :, start_block:start_block + CHIPS_ALL] for start_block in range(CHIP_LEN // SPACING)], axis=3)
        row_start = (row_first + offsets[0] + MARGIN).astype(jnp.int32)
        col_start = (SPACING * jnp.arange(CHIPS_ALL, dtype=jnp.int32) - REF_RIM + offsets[1] + MARGIN).astype(jnp.int32)

        def cut_chip(row_first_one, col_first_one):
            return lax.dynamic_slice(sec_pad, (jnp.int32(0), row_first_one, col_first_one), (2, CHIP_LEN, CHIP_LEN))
        sec_chips = jax.vmap(cut_chip)(row_start, col_start).transpose(1, 2, 0, 3)
        ref_re, ref_im = spectrum(ref_chips[0].astype(jnp.float32), ref_chips[1].astype(jnp.float32), four_re, four_im)
        sec_re, sec_im = spectrum(sec_chips[0].astype(jnp.float32), sec_chips[1].astype(jnp.float32), four_re, four_im)
        cross_re = rounded(ref_re * sec_re + ref_im * sec_im)
        cross_im = rounded(ref_im * sec_re - ref_re * sec_im)
        mid_re = rounded(jnp.einsum('pgq,vq->pgv', cross_re, lift_re) - jnp.einsum('pgq,vq->pgv', cross_im, lift_im))
        mid_im = rounded(jnp.einsum('pgq,vq->pgv', cross_re, lift_im) + jnp.einsum('pgq,vq->pgv', cross_im, lift_re))
        corr_re = jnp.einsum('up,pgv->ugv', lift_re, mid_re) - jnp.einsum('up,pgv->ugv', lift_im, mid_im)
        corr_im = jnp.einsum('up,pgv->ugv', lift_re, mid_im) + jnp.einsum('up,pgv->ugv', lift_im, mid_re)
        energy = corr_re * corr_re + corr_im * corr_im
        weight_map = energy * energy
        totals = lax.optimization_barrier(jnp.sum(weight_map, axis=(0, 2))) + EPS
        cent_az = jnp.einsum('u,ugv->g', lag_values, weight_map) / totals
        cent_rg = jnp.einsum('v,ugv->g', lag_values, weight_map) / totals
        return jnp.stack([offsets[0].astype(jnp.float32) + cent_az, offsets[1].astype(jnp.float32) + cent_rg])
    est_tiles = lax.map(per_tile, jnp.arange(TILES_AZ, dtype=jnp.int32))
    est_offsets = jnp.transpose(est_tiles, (1, 0, 2))
    line_data = jnp.take(secondary_slc, src_row, axis=1)
    padded_lines = jnp.pad(line_data, ((0, 0), (0, 0), (MARGIN, MARGIN)))
    summed = jnp.zeros((2, ALL_LINES, ALL_COLUMNS), jnp.float32)
    for tap_index in range(TAP_COUNT):
        picked = jnp.take(padded_lines, (band_start + tap_index + MARGIN).astype(jnp.int32), axis=2).astype(jnp.float32)
        summed = summed + picked * band_taps[tap_index].astype(jnp.float32)[None, None, :]
    field_rows = jnp.take(est_offsets[0], (src_row // LINES_DEV).astype(jnp.int32), axis=0)
    phase_angle = PHASE_RATE * jnp.repeat(field_rows, SPACING, axis=1)
    cosine = jnp.cos(phase_angle)
    sine_part = jnp.sin(phase_angle)
    line_re = summed[0] * cosine + summed[1] * sine_part
    line_im = summed[1] * cosine - summed[0] * sine_part
    lines_done = jnp.stack([line_re, line_im]).astype(jnp.bfloat16)
    line_ids = jnp.arange(ALL_LINES, dtype=jnp.int32)
    same_owner = line_owner[:, None] == line_owner[None, :]
    earlier = line_ids[:, None] > line_ids[None, :]
    own_rank = lax.optimization_barrier(jnp.sum((same_owner & earlier).astype(jnp.int32), axis=1))
    position = (line_owner * OWNER_CAP + own_rank).astype(jnp.int32)
    resampled = jnp.zeros((2, OWNERS * OWNER_CAP, ALL_COLUMNS), jnp.bfloat16).at[:, position, :].set(lines_done)
    return (est_offsets, resampled)
```

```python
import functools
import math

import jax
import jax.numpy as jnp
import numpy as np
from jax import lax
from jax.experimental import pallas as pl
from jax.experimental.pallas import tpu as pltpu
from jax.sharding import PartitionSpec as P

CHIP_LEN = 64
OVERSAMPLE = 16
LAG_COUNT = 48
TAP_COUNT = 8
SPACING = 32
MARGIN = 64
MAX_SHIFT = 8
LANES = 128
GROUP = 8

PHASE_RATE = 2.0
EPS = 1e-06
VMEM_LIMIT = 56 * 1024 * 1024


def shifted(cells, axis, up):
    count = lax.axis_size(axis)
    if up:
        pairs = [(i, i + 1) for i in range(count - 1)]
    else:
        pairs = [(i + 1, i) for i in range(count - 1)]
    return lax.ppermute(cells, axis, pairs)


def make_tables():
    indices = np.arange(CHIP_LEN)
    product = indices[:, None] * indices[None, :] % CHIP_LEN
    angles = (-2.0 * math.pi / CHIP_LEN) * product
    scaling = 1.0 / math.sqrt(CHIP_LEN)
    four_re = np.cos(angles) * scaling
    four_im = np.sin(angles) * scaling
    lag_steps = np.arange(LAG_COUNT) - LAG_COUNT // 2
    frequency = np.where(indices < CHIP_LEN // 2, indices, indices - CHIP_LEN)
    phase_turns = lag_steps[:, None] * frequency[None, :] % (OVERSAMPLE * CHIP_LEN)
    lifted = 2.0 * math.pi / (OVERSAMPLE * CHIP_LEN) * phase_turns
    lift_re = np.cos(lifted) * scaling
    lift_im = np.sin(lifted) * scaling
    lag_values = (lag_steps / OVERSAMPLE).astype(np.float32)

    def left(re, im):
        return np.block([[re, -im], [im, re]])

    def right(re, im):
        pad = ((0, CHIP_LEN - re.shape[0]), (0, 0))
        re2 = np.kron(np.eye(2), np.pad(re, pad).T)
        im2 = np.kron(np.eye(2), np.pad(im, pad).T)
        return np.block([[re2, im2], [-im2, re2]])

    def held(table):
        return jnp.asarray(table.astype(np.float32)).astype(jnp.bfloat16)

    return (
        held(left(four_re, four_im)),
        held(right(four_re, four_im)),
        held(right(lift_re, lift_im)),
        held(left(lift_re, lift_im)),
        lag_values,
    )


def dot(a, b):
    return jnp.dot(a, b, preferred_element_type=jnp.float32)


def gather_kernel(pick_ref, rows_ref, out_ref):
    lines = rows_ref.shape[1]
    rows = jnp.concatenate([rows_ref[0], rows_ref[1]], axis=0)
    out_ref[...] = dot(pick_ref[...], rows).astype(jnp.bfloat16)


def gather_rows(pick, rows):
    width = 1024
    while rows.shape[2] % width:
        width //= 2
    return pl.pallas_call(
        gather_kernel,
        grid=(rows.shape[2] // width,),
        in_specs=[
            pl.BlockSpec(pick.shape, lambda i: (0, 0)),
            pl.BlockSpec((2, rows.shape[1], width), lambda i: (0, 0, i)),
        ],
        out_specs=pl.BlockSpec((pick.shape[0], width), lambda i: (0, i)),
        out_shape=jax.ShapeDtypeStruct((pick.shape[0], rows.shape[2]), jnp.bfloat16),
        name="gather_rows",
    )(pick, rows)


def band_kernel(rel_ref, taps_ref, out_ref):
    blocks = out_ref.shape[0]
    place = lax.broadcasted_iota(jnp.int32, (2 * LANES, LANES), 0)
    for b in range(blocks):
        cols = pl.ds(b * LANES, LANES)
        delta = place - rel_ref[0:1, cols]
        taps = taps_ref[:, cols].astype(jnp.float32)
        band = jnp.zeros((2 * LANES, LANES), jnp.float32)
        for t in range(TAP_COUNT):
            band = jnp.where(delta == t, taps[t : t + 1], band)
        out_ref[b] = band.astype(jnp.bfloat16)


def build_bands(rel, taps):
    count = rel.shape[1] // LANES
    step = 8
    return pl.pallas_call(
        band_kernel,
        grid=(count // step,),
        in_specs=[
            pl.BlockSpec((1, step * LANES), lambda i: (0, i)),
            pl.BlockSpec((TAP_COUNT, step * LANES), lambda i: (0, i)),
        ],
        out_specs=pl.BlockSpec((step, 2 * LANES, LANES), lambda i: (i, 0, 0)),
        out_shape=jax.ShapeDtypeStruct((count, 2 * LANES, LANES), jnp.bfloat16),
        cost_estimate=pl.CostEstimate(
            flops=count * 2 * LANES * LANES * 32, bytes_accessed=count * 65536, transcendentals=0
        ),
        name="build_bands",
    )(rel, taps)


def estimate_kernel(
    off_ref, ref_ref, ref_left, ref_right, sec_ref, sec_top, sec_low, sec_left, sec_right,
    four_ref, spec_ref, lift_ref, corr_ref, lag_ref, out_ref, ref_win, sec_win,
):
    lines = sec_ref.shape[1]
    cols = sec_ref.shape[2]
    chips = cols // SPACING
    rim = (CHIP_LEN - SPACING) // 2
    first = lines // 2 - CHIP_LEN // 2
    f32 = jnp.float32
    blocks = cols // LANES
    high = MARGIN + lines
    for c in range(2):
        for b in range(blocks):
            at = slice(b * LANES, (b + 1) * LANES)
            ref_win[c, b + 1] = ref_ref[c, first : first + CHIP_LEN, at].astype(f32)
            sec_win[c, b + 1, :MARGIN] = sec_top[c, :, at].astype(f32)
            sec_win[c, b + 1, MARGIN:high] = sec_ref[c, :, at].astype(f32)
            sec_win[c, b + 1, high:] = sec_low[c, :, at].astype(f32)
        ref_win[c, 0, :, LANES - rim :] = ref_left[c].astype(f32)
        ref_win[c, blocks + 1, :, :rim] = ref_right[c].astype(f32)
        sec_win[c, 0, :, LANES - MARGIN :] = sec_left[c].astype(f32)
        sec_win[c, blocks + 1, :, :MARGIN] = sec_right[c].astype(f32)
    lane = lax.broadcasted_iota(jnp.int32, (CHIP_LEN, LANES), 1)

    def placed(win, c, row, col, half):
        block = col // LANES
        inner = col - block * LANES
        near = win[c, block, pl.ds(row, CHIP_LEN), :]
        far = win[c, block + 1, pl.ds(row, CHIP_LEN), :]
        turn = (half * CHIP_LEN - inner + LANES) % LANES
        near = pltpu.roll(near, turn, 1)
        far = pltpu.roll(far, turn, 1)
        return jnp.where(lane - half * CHIP_LEN + inner < LANES, near, far)

    def pair(win, rows, cols_at):
        parts = []
        for c in range(2):
            even = placed(win, c, rows[0], cols_at[0], 0)
            odd = placed(win, c, rows[1], cols_at[1], 1)
            parts.append(jnp.where(lane < CHIP_LEN, even, odd).astype(jnp.bfloat16))
        return jnp.concatenate(parts, axis=0)

    def step(i, carry):
        ref_chips, sec_chips = [], []
        for j in range(GROUP):
            g = (i * GROUP + j) * 2
            at = [LANES + SPACING * (g + h) - rim for h in range(2)]
            ref_chips.append(pair(ref_win, (0, 0), at))
            rows = [MARGIN + first + off_ref[0, g + h] for h in range(2)]
            sec_chips.append(pair(sec_win, rows, [at[h] + off_ref[1, g + h] for h in range(2)]))
        both = jnp.concatenate(ref_chips + sec_chips, axis=1)
        half = dot(four_ref[...], both).astype(jnp.bfloat16)
        lhs = jnp.concatenate(
            [
                jnp.concatenate(
                    [
                        half[:CHIP_LEN, j * LANES : (j + 1) * LANES],
                        half[CHIP_LEN:, j * LANES : (j + 1) * LANES],
                    ],
                    axis=1,
                )
                for j in range(2 * GROUP)
            ],
            axis=0,
        )
        spec = dot(lhs, spec_ref[...])
        rows = GROUP * CHIP_LEN
        rr, ri = spec[:rows, :LANES], spec[:rows, LANES:]
        sr, si = spec[rows:, :LANES], spec[rows:, LANES:]
        cross = jnp.concatenate([rr * sr + ri * si, ri * sr - rr * si], axis=1)
        mid = dot(cross.astype(jnp.bfloat16), lift_ref[...]).astype(jnp.bfloat16)
        tall = jnp.concatenate(
            [
                jnp.concatenate(
                    [
                        mid[j * CHIP_LEN : (j + 1) * CHIP_LEN, :LANES],
                        mid[j * CHIP_LEN : (j + 1) * CHIP_LEN, LANES:],
                    ],
                    axis=0,
                )
                for j in range(GROUP)
            ],
            axis=1,
        )
        corr = dot(corr_ref[...], tall)
        energy = corr[:LAG_COUNT] * corr[:LAG_COUNT] + corr[LAG_COUNT:] * corr[LAG_COUNT:]
        weight = energy * energy
        plain = jnp.sum(weight, axis=0, keepdims=True)
        lagged = jnp.sum(weight * lag_ref[...], axis=0, keepdims=True)
        out_ref[i] = jnp.concatenate([plain, lagged], axis=0)
        return carry

    lax.fori_loop(0, chips // (2 * GROUP), step, 0)


def estimate_sums(offsets, ref, ref_sides, sec, sec_rows, sec_sides, tables):
    four, spec, lift, corr, lags = tables
    cols = sec.shape[2]
    lines = sec.shape[1]
    chips = cols // SPACING
    steps = chips // (2 * GROUP)
    vmem = pl.BlockSpec(memory_space=pltpu.VMEM)
    blocks = cols // LANES + 3
    return pl.pallas_call(
        estimate_kernel,
        in_specs=[pl.BlockSpec(memory_space=pltpu.SMEM)] + [vmem] * 13,
        out_specs=vmem,
        out_shape=jax.ShapeDtypeStruct((steps, 2, GROUP * LANES), jnp.float32),
        scratch_shapes=[
            pltpu.VMEM((2, blocks, CHIP_LEN, LANES), jnp.float32),
            pltpu.VMEM((2, blocks, lines + 2 * MARGIN, LANES), jnp.float32),
        ],
        compiler_params=pltpu.CompilerParams(vmem_limit_bytes=VMEM_LIMIT),
        cost_estimate=pl.CostEstimate(
            flops=20_000_000_000, bytes_accessed=8_000_000, transcendentals=0
        ),
        name="estimate_sums",
    )(offsets, ref, *ref_sides, sec, *sec_rows, *sec_sides, four, spec, lift, corr,
      jnp.asarray(lags)[:, None])


def finish_kernel(pick_ref, rows_ref, band_ref, turn_ref, out_ref, wide):
    owned = out_ref.shape[1]
    piece = rows_ref.shape[1]
    count = wide.shape[1] // piece
    total = count * piece
    at = pl.program_id(0)

    @pl.when(at == 0)
    def _():
        wide[:, :MARGIN] = jnp.zeros((2 * owned, MARGIN), jnp.bfloat16)
        wide[:, MARGIN + total : 2 * MARGIN + total] = jnp.zeros((2 * owned, MARGIN), jnp.bfloat16)
        for r in range(count):
            lines = dot(pick_ref[pl.ds(r * 2 * owned, 2 * owned), :], rows_ref[...])
            wide[:, MARGIN + r * piece : MARGIN + (r + 1) * piece] = lines.astype(jnp.bfloat16)

    spread = 2 * LANES // SPACING
    lane = lax.broadcasted_iota(jnp.int32, (2 * spread, 2 * LANES), 1) // SPACING
    chip = lax.broadcasted_iota(jnp.int32, (2 * spread, 2 * LANES), 0) % spread
    expand = (lane == chip).astype(jnp.bfloat16)
    first = at * piece
    for b in range(piece // (2 * LANES)):
        turn = dot(turn_ref[0, b], expand)
        for h in range(2):
            k = 2 * b + h
            window = wide[:, pl.ds(pl.multiple_of(first + k * LANES, LANES), 2 * LANES)]
            s = dot(window, band_ref[k])
            cosine = turn[:owned, h * LANES : (h + 1) * LANES]
            sine = turn[owned:, h * LANES : (h + 1) * LANES]
            s_re, s_im = s[:owned], s[owned:]
            out_ref[0, :, k * LANES : (k + 1) * LANES] = (s_re * cosine + s_im * sine).astype(
                jnp.bfloat16
            )
            out_ref[1, :, k * LANES : (k + 1) * LANES] = (s_im * cosine - s_re * sine).astype(
                jnp.bfloat16
            )


def finish(pick, rows, bands, turns, owner_cap):
    piece = rows.shape[1]
    count = turns.shape[0]
    blocks = piece // LANES
    return pl.pallas_call(
        finish_kernel,
        grid=(count,),
        in_specs=[
            pl.BlockSpec(pick.shape, lambda i: (0, 0)),
            pl.BlockSpec(rows.shape, lambda i: (0, 0)),
            pl.BlockSpec((blocks, 2 * LANES, LANES), lambda i: (i, 0, 0)),
            pl.BlockSpec((1,) + turns.shape[1:], lambda i: (i, 0, 0, 0)),
        ],
        out_specs=pl.BlockSpec((2, owner_cap, piece), lambda i: (0, 0, i)),
        out_shape=jax.ShapeDtypeStruct((2, owner_cap, count * piece), jnp.bfloat16),
        scratch_shapes=[pltpu.VMEM((2 * owner_cap, count * piece + 2 * MARGIN), jnp.bfloat16)],
        compiler_params=pltpu.CompilerParams(vmem_limit_bytes=VMEM_LIMIT),
        name="finish_lines",
    )(pick, rows, bands, turns)


def per_device(
    reference_slc, secondary_slc, chip_offsets, src_row, line_owner, band_start, band_taps
):
    tables = make_tables()
    lines_dev = secondary_slc.shape[1]
    cols_dev = secondary_slc.shape[2]
    chip_count = cols_dev // SPACING
    az_count = lax.axis_size("az")
    rg_count = lax.axis_size("rg")
    owners = az_count * rg_count
    pair_cap = max(2, (lines_dev + 2 * MAX_SHIFT + owners - 1) // owners)
    owner_cap = pair_cap * az_count
    total_cols = cols_dev * rg_count
    rim = (CHIP_LEN - SPACING) // 2
    first_row = lines_dev // 2 - CHIP_LEN // 2
    az_index = lax.axis_index("az")
    rg_index = lax.axis_index("rg")
    me_owner = az_index * rg_count + rg_index

    count = src_row.shape[0]
    ids = jnp.arange(count, dtype=jnp.int32)
    src_tile = src_row // lines_dev
    mine = (line_owner[:, None] == line_owner[None, :]) & (ids[:, None] < ids[None, :])
    own_rank = jnp.sum(mine.astype(jnp.int32), axis=0)
    near = mine & (src_tile[:, None] == src_tile[None, :])
    pair_rank = jnp.sum(near.astype(jnp.int32), axis=0)

    local_row = src_row - az_index * lines_dev
    slot = jnp.where(src_tile == az_index, line_owner * pair_cap + pair_rank, -1)
    slots = jnp.arange(owners * pair_cap, dtype=jnp.int32)
    send_row = jnp.sum(
        jnp.where(slots[:, None] == slot[None, :], local_row[None, :] + 1, 0), axis=1
    ) - 1
    send_row = send_row.reshape(owners, 1, pair_cap)
    part = jnp.arange(2, dtype=jnp.int32)[None, :, None] * lines_dev
    target = jnp.where(send_row >= 0, send_row + part, -1).reshape(-1)
    send_pick = (
        target[:, None] == jnp.arange(2 * lines_dev, dtype=jnp.int32)[None, :]
    ).astype(jnp.bfloat16)
    outgoing = gather_rows(send_pick, secondary_slc)
    arrived = lax.all_to_all(outgoing, ("az", "rg"), split_axis=0, concat_axis=0, tiled=True)

    ref_rows = reference_slc[:, first_row : first_row + CHIP_LEN, :]
    ref_sides = (
        shifted(ref_rows[:, :, cols_dev - rim :], "rg", True),
        shifted(ref_rows[:, :, :rim], "rg", False),
    )
    sec_rows = (
        shifted(secondary_slc[:, lines_dev - MARGIN :, :], "az", True),
        shifted(secondary_slc[:, :MARGIN, :], "az", False),
    )
    tall_right = jnp.concatenate(
        [a[:, :, cols_dev - MARGIN :] for a in (sec_rows[0], secondary_slc, sec_rows[1])], axis=1
    )
    tall_left = jnp.concatenate(
        [a[:, :, :MARGIN] for a in (sec_rows[0], secondary_slc, sec_rows[1])], axis=1
    )
    sec_sides = (shifted(tall_right, "rg", True), shifted(tall_left, "rg", False))

    offsets = chip_offsets[:, 0]
    sums = estimate_sums(
        offsets, reference_slc, ref_sides, secondary_slc, sec_rows, sec_sides, tables
    )
    sums = jnp.moveaxis(sums, 1, 0).reshape(2, chip_count, CHIP_LEN)
    lag_wide = jnp.asarray(np.pad(tables[4], (0, CHIP_LEN - LAG_COUNT)))
    totals = jnp.sum(sums[0], axis=1) + EPS
    cent_az = jnp.sum(sums[1], axis=1) / totals
    cent_rg = jnp.sum(sums[0] * lag_wide[None, :], axis=1) / totals
    est = jnp.stack([cent_az, cent_rg]) + offsets.astype(jnp.float32)
    everywhere = lax.all_to_all(
        jnp.broadcast_to(est[0][None], (owners, chip_count)),
        ("az", "rg"),
        split_axis=0,
        concat_axis=0,
        tiled=True,
    ).reshape(az_count, rg_count, chip_count)

    all_cols = jnp.arange(total_cols, dtype=jnp.int32)
    rel = (band_start - all_cols // LANES * LANES + MARGIN)[None, :]
    bands = build_bands(rel, band_taps)

    outs = jnp.arange(owner_cap, dtype=jnp.int32)
    placed = (own_rank[None, :] == outs[:, None]) & (line_owner == me_owner)[None, :]
    which = jnp.sum(
        jnp.where(placed, (src_tile * pair_cap + pair_rank + 1)[None, :], 0), axis=1
    ) - 1
    tile = which // pair_cap
    from_rank = which % pair_cap
    rg_ids = jnp.arange(rg_count, dtype=jnp.int32)[:, None, None]
    parts = jnp.arange(2, dtype=jnp.int32)[None, :, None]
    source = ((tile[None, None] * rg_count + rg_ids) * 2 + parts) * pair_cap + from_rank[None, None]
    source = jnp.where(which[None, None] >= 0, source, -1).reshape(-1)
    recv_pick = (
        source[:, None] == jnp.arange(owners * 2 * pair_cap, dtype=jnp.int32)[None, :]
    ).astype(jnp.bfloat16)

    tiles = jnp.arange(az_count, dtype=jnp.int32)
    chosen = jnp.sum(
        jnp.where(
            (tile[:, None] == tiles[None, :])[:, :, None, None], everywhere[None], 0.0
        ),
        axis=1,
    )
    angle = PHASE_RATE * chosen
    spread = 2 * LANES // SPACING
    turns = jnp.stack([jnp.cos(angle), jnp.sin(angle)])
    high = turns.astype(jnp.bfloat16)
    low = (turns - high.astype(jnp.float32)).astype(jnp.bfloat16)
    turns = jnp.stack([high, low], axis=0).reshape(
        2, 2, owner_cap, rg_count, chip_count // spread, spread
    )
    turns = turns.transpose(3, 4, 1, 2, 0, 5).reshape(
        rg_count, chip_count // spread, 2 * owner_cap, 2 * spread
    )
    lines_out = finish(recv_pick, arrived, bands, turns, owner_cap)
    return (est[:, None, :], lines_out)


def solution(mesh):
    return jax.shard_map(
        per_device,
        mesh=mesh,
        in_specs=(
            P(None, "az", "rg"),
            P(None, "az", "rg"),
            P(None, "az", "rg"),
            P(),
            P(),
            P(),
            P(),
        ),
        out_specs=(P(None, "az", "rg"), P(None, ("az", "rg"), None)),
        check_vma=False,
    )
```

```python
import functools
import math

import jax
import jax.numpy as jnp
import numpy as np
from jax import lax
from jax.experimental import pallas as pl
from jax.experimental.pallas import tpu as pltpu
from jax.sharding import PartitionSpec as P

CHIP_LEN = 64
OVERSAMPLE = 16
LAG_COUNT = 48
TAP_COUNT = 8
SPACING = 32
MARGIN = 64
MAX_SHIFT = 8
LANES = 128
GROUP = 8

PHASE_RATE = 2.0
EPS = 1e-06
VMEM_LIMIT = 56 * 1024 * 1024


def moved(cells, az_step, rg_step):
    az_count = lax.axis_size("az")
    rg_count = lax.axis_size("rg")
    pairs = [
        (a * rg_count + r, (a + az_step) * rg_count + r + rg_step)
        for a in range(az_count)
        for r in range(rg_count)
        if 0 <= a + az_step < az_count and 0 <= r + rg_step < rg_count
    ]
    return lax.ppermute(cells, ("az", "rg"), pairs)


def make_tables():
    indices = np.arange(CHIP_LEN)
    product = indices[:, None] * indices[None, :] % CHIP_LEN
    angles = (-2.0 * math.pi / CHIP_LEN) * product
    scaling = 1.0 / math.sqrt(CHIP_LEN)
    four_re = np.cos(angles) * scaling
    four_im = np.sin(angles) * scaling
    lag_steps = np.arange(LAG_COUNT) - LAG_COUNT // 2
    frequency = np.where(indices < CHIP_LEN // 2, indices, indices - CHIP_LEN)
    phase_turns = lag_steps[:, None] * frequency[None, :] % (OVERSAMPLE * CHIP_LEN)
    lifted = 2.0 * math.pi / (OVERSAMPLE * CHIP_LEN) * phase_turns
    lift_re = np.cos(lifted) * scaling
    lift_im = np.sin(lifted) * scaling
    lag_values = (lag_steps / OVERSAMPLE).astype(np.float32)

    def left(re, im):
        return np.block([[re, -im], [im, re]])

    def right(re, im):
        pad = ((0, CHIP_LEN - re.shape[0]), (0, 0))
        re2 = np.kron(np.eye(2), np.pad(re, pad).T)
        im2 = np.kron(np.eye(2), np.pad(im, pad).T)
        return np.block([[re2, im2], [-im2, re2]])

    def held(table):
        return jnp.asarray(table.astype(np.float32)).astype(jnp.bfloat16)

    return (
        held(left(four_re, four_im)),
        held(right(four_re, four_im)),
        held(right(lift_re, lift_im)),
        held(left(lift_re, lift_im)),
        lag_values,
    )


def dot(a, b):
    return jnp.dot(a, b, preferred_element_type=jnp.float32)


def gather_kernel(pick_ref, rows_ref, out_ref):
    lines = rows_ref.shape[1]
    rows = jnp.concatenate([rows_ref[0], rows_ref[1]], axis=0)
    out_ref[...] = dot(pick_ref[...], rows).astype(jnp.bfloat16)


def gather_rows(pick, rows):
    width = 1024
    while rows.shape[2] % width:
        width //= 2
    return pl.pallas_call(
        gather_kernel,
        grid=(rows.shape[2] // width,),
        in_specs=[
            pl.BlockSpec(pick.shape, lambda i: (0, 0)),
            pl.BlockSpec((2, rows.shape[1], width), lambda i: (0, 0, i)),
        ],
        out_specs=pl.BlockSpec((pick.shape[0], width), lambda i: (0, i)),
        out_shape=jax.ShapeDtypeStruct((pick.shape[0], rows.shape[2]), jnp.bfloat16),
        name="gather_rows",
    )(pick, rows)


def band_kernel(rel_ref, taps_ref, out_ref):
    blocks = out_ref.shape[0]
    place = lax.broadcasted_iota(jnp.int32, (2 * LANES, LANES), 0)
    for b in range(blocks):
        cols = pl.ds(b * LANES, LANES)
        delta = place - rel_ref[0:1, cols]
        taps = taps_ref[:, cols].astype(jnp.float32)
        band = jnp.zeros((2 * LANES, LANES), jnp.float32)
        for t in range(TAP_COUNT):
            band = jnp.where(delta == t, taps[t : t + 1], band)
        out_ref[b] = band.astype(jnp.bfloat16)


def build_bands(rel, taps):
    count = rel.shape[1] // LANES
    step = 8
    return pl.pallas_call(
        band_kernel,
        grid=(count // step,),
        in_specs=[
            pl.BlockSpec((1, step * LANES), lambda i: (0, i)),
            pl.BlockSpec((TAP_COUNT, step * LANES), lambda i: (0, i)),
        ],
        out_specs=pl.BlockSpec((step, 2 * LANES, LANES), lambda i: (i, 0, 0)),
        out_shape=jax.ShapeDtypeStruct((count, 2 * LANES, LANES), jnp.bfloat16),
        cost_estimate=pl.CostEstimate(
            flops=count * 2 * LANES * LANES * 32, bytes_accessed=count * 65536, transcendentals=0
        ),
        name="build_bands",
    )(rel, taps)


def estimate_kernel(
    off_ref, ref_ref, sec_ref, sec_top, sec_low, left, right, top_left, top_right, low_left,
    low_right, four_ref, spec_ref, lift_ref, corr_ref, lag_ref, wide_ref, out_ref, ref_win,
    sec_win, plain_ref, lagged_ref,
):
    lines = sec_ref.shape[1]
    cols = sec_ref.shape[2]
    chips = cols // SPACING
    rim = (CHIP_LEN - SPACING) // 2
    first = lines // 2 - CHIP_LEN // 2
    f32 = jnp.float32
    blocks = cols // LANES
    high = MARGIN + lines
    for c in range(2):
        for b in range(blocks):
            at = slice(b * LANES, (b + 1) * LANES)
            ref_win[c, b + 1] = ref_ref[c, first : first + CHIP_LEN, at].astype(f32)
            sec_win[c, b + 1, :MARGIN] = sec_top[c, :, at].astype(f32)
            sec_win[c, b + 1, MARGIN:high] = sec_ref[c, :, at].astype(f32)
            sec_win[c, b + 1, high:] = sec_low[c, :, at].astype(f32)
        ref_win[c, 0, :, LANES - MARGIN :] = left[c, lines:].astype(f32)
        ref_win[c, blocks + 1, :, :MARGIN] = right[c, lines:].astype(f32)
        sec_win[c, 0, :MARGIN, LANES - MARGIN :] = top_left[c].astype(f32)
        sec_win[c, 0, MARGIN:high, LANES - MARGIN :] = left[c, :lines].astype(f32)
        sec_win[c, 0, high:, LANES - MARGIN :] = low_left[c].astype(f32)
        sec_win[c, blocks + 1, :MARGIN, :MARGIN] = top_right[c].astype(f32)
        sec_win[c, blocks + 1, MARGIN:high, :MARGIN] = right[c, :lines].astype(f32)
        sec_win[c, blocks + 1, high:, :MARGIN] = low_right[c].astype(f32)
    lane = lax.broadcasted_iota(jnp.int32, (CHIP_LEN, LANES), 1)

    def placed(win, c, row, col, half):
        block = col // LANES
        inner = col - block * LANES
        near = win[c, block, pl.ds(row, CHIP_LEN), :]
        far = win[c, block + 1, pl.ds(row, CHIP_LEN), :]
        turn = (half * CHIP_LEN - inner + LANES) % LANES
        near = pltpu.roll(near, turn, 1)
        far = pltpu.roll(far, turn, 1)
        return jnp.where(lane - half * CHIP_LEN + inner < LANES, near, far)

    def pair(win, rows, cols_at):
        parts = []
        for c in range(2):
            even = placed(win, c, rows[0], cols_at[0], 0)
            odd = placed(win, c, rows[1], cols_at[1], 1)
            parts.append(jnp.where(lane < CHIP_LEN, even, odd).astype(jnp.bfloat16))
        return jnp.concatenate(parts, axis=0)

    def step(i, carry):
        ref_chips, sec_chips = [], []
        for j in range(GROUP):
            g = (i * GROUP + j) * 2
            at = [LANES + SPACING * (g + h) - rim for h in range(2)]
            ref_chips.append(pair(ref_win, (0, 0), at))
            rows = [MARGIN + first + off_ref[0, g + h] for h in range(2)]
            sec_chips.append(pair(sec_win, rows, [at[h] + off_ref[1, g + h] for h in range(2)]))
        both = jnp.concatenate(ref_chips + sec_chips, axis=1)
        half = dot(four_ref[...], both).astype(jnp.bfloat16)
        lhs = jnp.concatenate(
            [
                jnp.concatenate(
                    [
                        half[:CHIP_LEN, j * LANES : (j + 1) * LANES],
                        half[CHIP_LEN:, j * LANES : (j + 1) * LANES],
                    ],
                    axis=1,
                )
                for j in range(2 * GROUP)
            ],
            axis=0,
        )
        spec = dot(lhs, spec_ref[...])
        rows = GROUP * CHIP_LEN
        rr, ri = spec[:rows, :LANES], spec[:rows, LANES:]
        sr, si = spec[rows:, :LANES], spec[rows:, LANES:]
        cross = jnp.concatenate([rr * sr + ri * si, ri * sr - rr * si], axis=1)
        mid = dot(cross.astype(jnp.bfloat16), lift_ref[...]).astype(jnp.bfloat16)
        tall = jnp.concatenate(
            [
                jnp.concatenate(
                    [
                        mid[j * CHIP_LEN : (j + 1) * CHIP_LEN, :LANES],
                        mid[j * CHIP_LEN : (j + 1) * CHIP_LEN, LANES:],
                    ],
                    axis=0,
                )
                for j in range(GROUP)
            ],
            axis=1,
        )
        corr = dot(corr_ref[...], tall)
        energy = corr[:LAG_COUNT] * corr[:LAG_COUNT] + corr[LAG_COUNT:] * corr[LAG_COUNT:]
        weight = energy * energy
        plain = jnp.sum(weight, axis=0, keepdims=True)
        lagged = jnp.sum(weight * lag_ref[...], axis=0, keepdims=True)
        for j in range(GROUP):
            at = slice(j * LANES, (j + 1) * LANES)
            plain_ref[pl.ds(i * GROUP + j, 1), :] = plain[:, at]
            lagged_ref[pl.ds(i * GROUP + j, 1), :] = lagged[:, at]
        return carry

    lax.fori_loop(0, chips // (2 * GROUP), step, 0)
    near = lax.broadcasted_iota(jnp.int32, (chips // 2, LANES), 1) < CHIP_LEN
    plain = plain_ref[...]
    lagged = lagged_ref[...]
    across = plain * wide_ref[...]
    for h in range(2):
        inside = near if h == 0 else jnp.logical_not(near)
        total = jnp.sum(jnp.where(inside, plain, 0.0), axis=1, keepdims=True) + EPS
        out_ref[0, :, h : h + 1] = (
            jnp.sum(jnp.where(inside, lagged, 0.0), axis=1, keepdims=True) / total
        )
        out_ref[1, :, h : h + 1] = (
            jnp.sum(jnp.where(inside, across, 0.0), axis=1, keepdims=True) / total
        )


def estimate_shifts(offsets, ref, sec, halos, tables):
    four, spec, lift, corr, lags = tables
    lines = sec.shape[1]
    chips = sec.shape[2] // SPACING
    vmem = pl.BlockSpec(memory_space=pltpu.VMEM)
    blocks = sec.shape[2] // LANES + 3
    lag_wide = np.tile(np.pad(lags, (0, CHIP_LEN - LAG_COUNT)), 2)[None, :]
    return pl.pallas_call(
        estimate_kernel,
        in_specs=[pl.BlockSpec(memory_space=pltpu.SMEM)] + [vmem] * 16,
        out_specs=vmem,
        out_shape=jax.ShapeDtypeStruct((2, chips // 2, 2), jnp.float32),
        scratch_shapes=[
            pltpu.VMEM((2, blocks, CHIP_LEN, LANES), jnp.float32),
            pltpu.VMEM((2, blocks, lines + 2 * MARGIN, LANES), jnp.float32),
            pltpu.VMEM((chips // 2, LANES), jnp.float32),
            pltpu.VMEM((chips // 2, LANES), jnp.float32),
        ],
        compiler_params=pltpu.CompilerParams(vmem_limit_bytes=VMEM_LIMIT),
        cost_estimate=pl.CostEstimate(
            flops=10_000_000_000, bytes_accessed=8_000_000, transcendentals=0
        ),
        name="estimate_shifts",
    )(offsets, ref, sec, *halos, four, spec, lift, corr, jnp.asarray(lags)[:, None],
      jnp.asarray(lag_wide))


def resample_kernel(pick_ref, rows_ref, band_ref, out_ref, wide):
    owned = out_ref.shape[1]
    piece = rows_ref.shape[1]
    count = (wide.shape[1] - 2 * MARGIN) // piece
    total = count * piece
    at = pl.program_id(0)

    @pl.when(at == 0)
    def _():
        wide[:, :MARGIN] = jnp.zeros((2 * owned, MARGIN), jnp.bfloat16)
        wide[:, MARGIN + total : 2 * MARGIN + total] = jnp.zeros((2 * owned, MARGIN), jnp.bfloat16)
        for r in range(count):
            lines = dot(pick_ref[pl.ds(r * 2 * owned, 2 * owned), :], rows_ref[...])
            wide[:, MARGIN + r * piece : MARGIN + (r + 1) * piece] = lines.astype(jnp.bfloat16)

    first = at * piece
    for k in range(piece // LANES):
        window = wide[:, pl.ds(pl.multiple_of(first + k * LANES, LANES), 2 * LANES)]
        s = dot(window, band_ref[k])
        out_ref[0, :, k * LANES : (k + 1) * LANES] = s[:owned]
        out_ref[1, :, k * LANES : (k + 1) * LANES] = s[owned:]


def resample(pick, rows, bands, owner_cap):
    piece = rows.shape[1]
    blocks = piece // LANES
    count = bands.shape[0] // blocks
    return pl.pallas_call(
        resample_kernel,
        grid=(count,),
        in_specs=[
            pl.BlockSpec(pick.shape, lambda i: (0, 0)),
            pl.BlockSpec(rows.shape, lambda i: (0, 0)),
            pl.BlockSpec((blocks, 2 * LANES, LANES), lambda i: (i, 0, 0)),
        ],
        out_specs=pl.BlockSpec((2, owner_cap, piece), lambda i: (0, 0, i)),
        out_shape=jax.ShapeDtypeStruct((2, owner_cap, count * piece), jnp.float32),
        scratch_shapes=[pltpu.VMEM((2 * owner_cap, count * piece + 2 * MARGIN), jnp.bfloat16)],
        compiler_params=pltpu.CompilerParams(vmem_limit_bytes=VMEM_LIMIT),
        cost_estimate=pl.CostEstimate(
            flops=6_000_000_000, bytes_accessed=12_000_000, transcendentals=0
        ),
        name="resample",
    )(pick, rows, bands)


def rotate_kernel(tile_ref, est_ref, lines_ref, out_ref):
    owned = out_ref.shape[1]
    count = pl.num_programs(0)
    at = pl.program_id(0)
    tiles = est_ref.shape[0] // count
    tile = tile_ref[...]
    shift = jnp.zeros((owned, LANES), jnp.float32)
    for a in range(tiles):
        shift = jnp.where(tile == a, est_ref[pl.ds(a * count + at, 1), :], shift)
    angle = PHASE_RATE * shift
    cosine = jnp.cos(angle)
    sine = jnp.sin(angle)
    lane = lax.broadcasted_iota(jnp.int32, (owned, LANES), 1) // SPACING
    for k in range(out_ref.shape[2] // LANES):
        chip = lane + k * (LANES // SPACING)
        cos_k = jnp.take_along_axis(cosine, chip, axis=1)
        sin_k = jnp.take_along_axis(sine, chip, axis=1)
        cols = slice(k * LANES, (k + 1) * LANES)
        s_re = lines_ref[0, :, cols]
        s_im = lines_ref[1, :, cols]
        out_ref[0, :, cols] = (s_re * cos_k + s_im * sin_k).astype(jnp.bfloat16)
        out_ref[1, :, cols] = (s_im * cos_k - s_re * sin_k).astype(jnp.bfloat16)


def rotate(tile, est, lines, count):
    piece = lines.shape[2] // count
    return pl.pallas_call(
        rotate_kernel,
        grid=(count,),
        in_specs=[
            pl.BlockSpec(tile.shape, lambda i: (0, 0)),
            pl.BlockSpec(est.shape, lambda i: (0, 0)),
            pl.BlockSpec((2, lines.shape[1], piece), lambda i: (0, 0, i)),
        ],
        out_specs=pl.BlockSpec((2, lines.shape[1], piece), lambda i: (0, 0, i)),
        out_shape=jax.ShapeDtypeStruct(lines.shape, jnp.bfloat16),
        name="rotate",
    )(tile, est, lines)


def per_device(
    reference_slc, secondary_slc, chip_offsets, src_row, line_owner, band_start, band_taps
):
    tables = make_tables()
    lines_dev = secondary_slc.shape[1]
    cols_dev = secondary_slc.shape[2]
    chip_count = cols_dev // SPACING
    az_count = lax.axis_size("az")
    rg_count = lax.axis_size("rg")
    owners = az_count * rg_count
    pair_cap = max(2, (lines_dev + 2 * MAX_SHIFT + owners - 1) // owners)
    owner_cap = pair_cap * az_count
    total_cols = cols_dev * rg_count
    first_row = lines_dev // 2 - CHIP_LEN // 2
    az_index = lax.axis_index("az")
    rg_index = lax.axis_index("rg")
    me_owner = az_index * rg_count + rg_index

    low_rows = secondary_slc[:, lines_dev - MARGIN :, :]
    top_rows = secondary_slc[:, :MARGIN, :]
    last = cols_dev - MARGIN
    edges = jnp.concatenate(
        [secondary_slc, reference_slc[:, first_row : first_row + CHIP_LEN, :]], axis=1
    )
    halos = (
        moved(low_rows, 1, 0),
        moved(top_rows, -1, 0),
        moved(edges[:, :, last:], 0, 1),
        moved(edges[:, :, :MARGIN], 0, -1),
        moved(low_rows[:, :, last:], 1, 1),
        moved(low_rows[:, :, :MARGIN], 1, -1),
        moved(top_rows[:, :, last:], -1, 1),
        moved(top_rows[:, :, :MARGIN], -1, -1),
    )

    count = src_row.shape[0]
    ids = jnp.arange(count, dtype=jnp.int32)
    src_tile = src_row // lines_dev
    mine = (line_owner[:, None] == line_owner[None, :]) & (ids[:, None] < ids[None, :])
    own_rank = jnp.sum(mine.astype(jnp.int32), axis=0)
    near = mine & (src_tile[:, None] == src_tile[None, :])
    pair_rank = jnp.sum(near.astype(jnp.int32), axis=0)

    local_row = src_row - az_index * lines_dev
    slot = jnp.where(src_tile == az_index, line_owner * pair_cap + pair_rank, -1)
    slots = jnp.arange(owners * pair_cap, dtype=jnp.int32)
    send_row = jnp.sum(
        jnp.where(slots[:, None] == slot[None, :], local_row[None, :] + 1, 0), axis=1
    ) - 1
    send_row = send_row.reshape(owners, 1, pair_cap)
    part = jnp.arange(2, dtype=jnp.int32)[None, :, None] * lines_dev
    target = jnp.where(send_row >= 0, send_row + part, -1).reshape(-1)
    send_pick = (
        target[:, None] == jnp.arange(2 * lines_dev, dtype=jnp.int32)[None, :]
    ).astype(jnp.bfloat16)
    outgoing = gather_rows(send_pick, secondary_slc)
    with jax.named_scope("exchange"):
        arrived = lax.all_to_all(
            outgoing, ("az", "rg"), split_axis=0, concat_axis=0, tiled=True
        )

    offsets = chip_offsets[:, 0]
    with jax.named_scope("estimate"):
        shifts = estimate_shifts(offsets, reference_slc, secondary_slc, halos, tables)
    est = shifts.reshape(2, chip_count) + offsets.astype(jnp.float32)
    with jax.named_scope("spread"):
        everywhere = lax.all_to_all(
            jnp.broadcast_to(jnp.pad(est[:1], ((0, 0), (0, LANES - chip_count))), (owners, LANES)),
            ("az", "rg"),
            split_axis=0,
            concat_axis=0,
            tiled=True,
        )

    all_cols = jnp.arange(total_cols, dtype=jnp.int32)
    rel = (band_start - all_cols // LANES * LANES + MARGIN)[None, :]
    bands = build_bands(rel, band_taps)

    outs = jnp.arange(owner_cap, dtype=jnp.int32)
    placed = (own_rank[None, :] == outs[:, None]) & (line_owner == me_owner)[None, :]
    which = jnp.sum(
        jnp.where(placed, (src_tile * pair_cap + pair_rank + 1)[None, :], 0), axis=1
    ) - 1
    tile = which // pair_cap
    from_rank = which % pair_cap
    rg_ids = jnp.arange(rg_count, dtype=jnp.int32)[:, None, None]
    parts = jnp.arange(2, dtype=jnp.int32)[None, :, None]
    source = ((tile[None, None] * rg_count + rg_ids) * 2 + parts) * pair_cap + from_rank[None, None]
    source = jnp.where(which[None, None] >= 0, source, -1).reshape(-1)
    recv_pick = (
        source[:, None] == jnp.arange(owners * 2 * pair_cap, dtype=jnp.int32)[None, :]
    ).astype(jnp.bfloat16)

    lines = resample(recv_pick, arrived, bands, owner_cap)
    tile_wide = jnp.broadcast_to(tile[:, None], (owner_cap, LANES))
    lines_out = rotate(tile_wide, everywhere, lines, rg_count)
    return (est[:, None, :], lines_out)


def solution(mesh):
    return jax.shard_map(
        per_device,
        mesh=mesh,
        in_specs=(
            P(None, "az", "rg"),
            P(None, "az", "rg"),
            P(None, "az", "rg"),
            P(),
            P(),
            P(),
            P(),
        ),
        out_specs=(P(None, "az", "rg"), P(None, ("az", "rg"), None)),
        check_vma=False,
    )
```

```python
import math

import jax
import jax.numpy as jnp
import numpy as np
from jax import lax
from jax.experimental import pallas as pl
from jax.experimental.pallas import tpu as pltpu
from jax.sharding import PartitionSpec as P


CHIP_LEN = 64
OVERSAMPLE = 16
LAG_COUNT = 48
TAP_COUNT = 8
SPACING = 32
MARGIN = 64
MAX_SHIFT = 8
LANES = 128
GROUP = 8

PHASE_RATE = 2.0
EPS = 1e-06
VMEM_LIMIT = 56 * 1024 * 1024


def moved(cells, az_step, rg_step):
    az_count = lax.axis_size("az")
    rg_count = lax.axis_size("rg")
    pairs = [
        (a * rg_count + r, (a + az_step) * rg_count + r + rg_step)
        for a in range(az_count)
        for r in range(rg_count)
        if 0 <= a + az_step < az_count and 0 <= r + rg_step < rg_count
    ]
    return lax.ppermute(cells, ("az", "rg"), pairs)


def make_tables():
    indices = np.arange(CHIP_LEN)
    product = indices[:, None] * indices[None, :] % CHIP_LEN
    angles = (-2.0 * math.pi / CHIP_LEN) * product
    scaling = 1.0 / math.sqrt(CHIP_LEN)
    four_re = np.cos(angles) * scaling
    four_im = np.sin(angles) * scaling
    lag_steps = np.arange(LAG_COUNT) - LAG_COUNT // 2
    frequency = np.where(indices < CHIP_LEN // 2, indices, indices - CHIP_LEN)
    phase_turns = lag_steps[:, None] * frequency[None, :] % (OVERSAMPLE * CHIP_LEN)
    lifted = 2.0 * math.pi / (OVERSAMPLE * CHIP_LEN) * phase_turns
    lift_re = np.cos(lifted) * scaling
    lift_im = np.sin(lifted) * scaling
    lag_values = (lag_steps / OVERSAMPLE).astype(np.float32)

    def left(re, im):
        return np.block([[re, -im], [im, re]])

    def right(re, im):
        pad = ((0, CHIP_LEN - re.shape[0]), (0, 0))
        re2 = np.kron(np.eye(2), np.pad(re, pad).T)
        im2 = np.kron(np.eye(2), np.pad(im, pad).T)
        return np.block([[re2, im2], [-im2, re2]])

    def held(table):
        return jnp.asarray(table.astype(np.float32)).astype(jnp.bfloat16)

    return (
        held(left(four_re, four_im)),
        held(right(four_re, four_im)),
        held(right(lift_re, lift_im)),
        held(left(lift_re, lift_im)),
        lag_values,
    )


def dot(a, b):
    return jnp.dot(a, b, preferred_element_type=jnp.float32)


def gather_kernel(pick_ref, rows_ref, out_ref):
    rows = jnp.concatenate([rows_ref[0], rows_ref[1]], axis=0)
    out_ref[...] = dot(pick_ref[...], rows).astype(jnp.bfloat16)


def gather_rows(pick, rows):
    width = 1024
    while rows.shape[2] % width:
        width //= 2
    return pl.pallas_call(
        gather_kernel,
        grid=(rows.shape[2] // width,),
        in_specs=[
            pl.BlockSpec(pick.shape, lambda i: (0, 0)),
            pl.BlockSpec((2, rows.shape[1], width), lambda i: (0, 0, i)),
        ],
        out_specs=pl.BlockSpec((pick.shape[0], width), lambda i: (0, i)),
        out_shape=jax.ShapeDtypeStruct((pick.shape[0], rows.shape[2]), jnp.bfloat16),
        name="gather_rows",
    )(pick, rows)


def band_kernel(rel_ref, taps_ref, out_ref):
    blocks = out_ref.shape[0]
    place = lax.broadcasted_iota(jnp.int32, (2 * LANES, LANES), 0)
    for b in range(blocks):
        cols = pl.ds(b * LANES, LANES)
        delta = place - rel_ref[0:1, cols]
        taps = taps_ref[:, cols].astype(jnp.float32)
        band = jnp.zeros((2 * LANES, LANES), jnp.float32)
        for t in range(TAP_COUNT):
            band = jnp.where(delta == t, taps[t : t + 1], band)
        out_ref[b] = band.astype(jnp.bfloat16)


def build_bands(rel, taps):
    count = rel.shape[1] // LANES
    step = 8
    return pl.pallas_call(
        band_kernel,
        grid=(count // step,),
        in_specs=[
            pl.BlockSpec((1, step * LANES), lambda i: (0, i)),
            pl.BlockSpec((TAP_COUNT, step * LANES), lambda i: (0, i)),
        ],
        out_specs=pl.BlockSpec((step, 2 * LANES, LANES), lambda i: (i, 0, 0)),
        out_shape=jax.ShapeDtypeStruct((count, 2 * LANES, LANES), jnp.bfloat16),
        cost_estimate=pl.CostEstimate(
            flops=count * 2 * LANES * LANES * 32, bytes_accessed=count * 65536, transcendentals=0
        ),
        name="build_bands",
    )(rel, taps)


def estimate_kernel(
    off_ref, ref_ref, sec_ref, sec_top, sec_low, left, right, top_left, top_right, low_left,
    low_right, four_ref, spec_ref, lift_ref, corr_ref, lag_ref, wide_ref, base_ref, out_ref,
    spread_ref, ref_win, sec_win, plain_ref, lagged_ref,
):
    lines = sec_ref.shape[1]
    cols = sec_ref.shape[2]
    chips = cols // SPACING
    rim = (CHIP_LEN - SPACING) // 2
    first = lines // 2 - CHIP_LEN // 2
    f32 = jnp.float32
    blocks = cols // LANES
    high = MARGIN + lines
    for c in range(2):
        for b in range(blocks):
            at = slice(b * LANES, (b + 1) * LANES)
            ref_win[c, b + 1] = ref_ref[c, first : first + CHIP_LEN, at].astype(f32)
            sec_win[c, b + 1, :MARGIN] = sec_top[c, :, at].astype(f32)
            sec_win[c, b + 1, MARGIN:high] = sec_ref[c, :, at].astype(f32)
            sec_win[c, b + 1, high:] = sec_low[c, :, at].astype(f32)
        ref_win[c, 0, :, LANES - MARGIN :] = left[c, lines:].astype(f32)
        ref_win[c, blocks + 1, :, :MARGIN] = right[c, lines:].astype(f32)
        sec_win[c, 0, :MARGIN, LANES - MARGIN :] = top_left[c].astype(f32)
        sec_win[c, 0, MARGIN:high, LANES - MARGIN :] = left[c, :lines].astype(f32)
        sec_win[c, 0, high:, LANES - MARGIN :] = low_left[c].astype(f32)
        sec_win[c, blocks + 1, :MARGIN, :MARGIN] = top_right[c].astype(f32)
        sec_win[c, blocks + 1, MARGIN:high, :MARGIN] = right[c, :lines].astype(f32)
        sec_win[c, blocks + 1, high:, :MARGIN] = low_right[c].astype(f32)
    lane = lax.broadcasted_iota(jnp.int32, (CHIP_LEN, LANES), 1)

    def placed(win, c, row, col, half):
        block = col // LANES
        inner = col - block * LANES
        near = win[c, block, pl.ds(row, CHIP_LEN), :]
        far = win[c, block + 1, pl.ds(row, CHIP_LEN), :]
        turn = (half * CHIP_LEN - inner + LANES) % LANES
        near = pltpu.roll(near, turn, 1)
        far = pltpu.roll(far, turn, 1)
        return jnp.where(lane - half * CHIP_LEN + inner < LANES, near, far)

    def pair(win, rows, cols_at):
        parts = []
        for c in range(2):
            even = placed(win, c, rows[0], cols_at[0], 0)
            odd = placed(win, c, rows[1], cols_at[1], 1)
            parts.append(jnp.where(lane < CHIP_LEN, even, odd).astype(jnp.bfloat16))
        return jnp.concatenate(parts, axis=0)

    def step(i, carry):
        ref_chips, sec_chips = [], []
        for j in range(GROUP):
            g = (i * GROUP + j) * 2
            at = [LANES + SPACING * (g + h) - rim for h in range(2)]
            ref_chips.append(pair(ref_win, (0, 0), at))
            rows = [MARGIN + first + off_ref[0, g + h] for h in range(2)]
            sec_chips.append(pair(sec_win, rows, [at[h] + off_ref[1, g + h] for h in range(2)]))
        both = jnp.concatenate(ref_chips + sec_chips, axis=1)
        half = dot(four_ref[...], both).astype(jnp.bfloat16)
        lhs = jnp.concatenate(
            [
                jnp.concatenate(
                    [
                        half[:CHIP_LEN, j * LANES : (j + 1) * LANES],
                        half[CHIP_LEN:, j * LANES : (j + 1) * LANES],
                    ],
                    axis=1,
                )
                for j in range(2 * GROUP)
            ],
            axis=0,
        )
        spec = dot(lhs, spec_ref[...])
        rows = GROUP * CHIP_LEN
        rr, ri = spec[:rows, :LANES], spec[:rows, LANES:]
        sr, si = spec[rows:, :LANES], spec[rows:, LANES:]
        cross = jnp.concatenate([rr * sr + ri * si, ri * sr - rr * si], axis=1)
        mid = dot(cross.astype(jnp.bfloat16), lift_ref[...]).astype(jnp.bfloat16)
        tall = jnp.concatenate(
            [
                jnp.concatenate(
                    [
                        mid[j * CHIP_LEN : (j + 1) * CHIP_LEN, :LANES],
                        mid[j * CHIP_LEN : (j + 1) * CHIP_LEN, LANES:],
                    ],
                    axis=0,
                )
                for j in range(GROUP)
            ],
            axis=1,
        )
        corr = dot(corr_ref[...], tall)
        energy = corr[:LAG_COUNT] * corr[:LAG_COUNT] + corr[LAG_COUNT:] * corr[LAG_COUNT:]
        weight = energy * energy
        plain = jnp.sum(weight, axis=0, keepdims=True)
        lagged = jnp.sum(weight * lag_ref[...], axis=0, keepdims=True)
        for j in range(GROUP):
            at = slice(j * LANES, (j + 1) * LANES)
            plain_ref[pl.ds(i * GROUP + j, 1), :] = plain[:, at]
            lagged_ref[pl.ds(i * GROUP + j, 1), :] = lagged[:, at]
        return carry

    lax.fori_loop(0, chips // (2 * GROUP), step, 0)
    near = lax.broadcasted_iota(jnp.int32, (chips // 2, LANES), 1) < CHIP_LEN
    plain = plain_ref[...]
    lagged = lagged_ref[...]
    across = plain * wide_ref[...]
    lane = lax.broadcasted_iota(jnp.int32, (chips // 2, LANES), 1)
    place = lax.broadcasted_iota(jnp.int32, (chips // 2, LANES), 0) * 2
    rows = [jnp.zeros((chips // 2, LANES), jnp.float32)] * 2
    for h in range(2):
        inside = near if h == 0 else jnp.logical_not(near)
        total = jnp.sum(jnp.where(inside, plain, 0.0), axis=1, keepdims=True) + EPS
        for c, moment in enumerate((lagged, across)):
            centre = jnp.sum(jnp.where(inside, moment, 0.0), axis=1, keepdims=True) / total
            rows[c] = jnp.where(lane == place + h, centre, rows[c])
    for c in range(2):
        out_ref[c : c + 1, :] = jnp.sum(rows[c], axis=0, keepdims=True) + base_ref[c : c + 1, :]
    spread_ref[...] = jnp.broadcast_to(out_ref[0:1, :], spread_ref.shape)


def estimate_shifts(offsets, ref, sec, halos, tables, owners):
    four, spec, lift, corr, lags = tables
    lines = sec.shape[1]
    chips = sec.shape[2] // SPACING
    vmem = pl.BlockSpec(memory_space=pltpu.VMEM)
    blocks = sec.shape[2] // LANES + 3
    lag_wide = np.tile(np.pad(lags, (0, CHIP_LEN - LAG_COUNT)), 2)[None, :]
    return pl.pallas_call(
        estimate_kernel,
        in_specs=[pl.BlockSpec(memory_space=pltpu.SMEM)] + [vmem] * 17,
        out_specs=(vmem, vmem),
        out_shape=(
            jax.ShapeDtypeStruct((2, LANES), jnp.float32),
            jax.ShapeDtypeStruct((owners, LANES), jnp.float32),
        ),
        scratch_shapes=[
            pltpu.VMEM((2, blocks, CHIP_LEN, LANES), jnp.float32),
            pltpu.VMEM((2, blocks, lines + 2 * MARGIN, LANES), jnp.float32),
            pltpu.VMEM((chips // 2, LANES), jnp.float32),
            pltpu.VMEM((chips // 2, LANES), jnp.float32),
        ],
        compiler_params=pltpu.CompilerParams(vmem_limit_bytes=VMEM_LIMIT),
        cost_estimate=pl.CostEstimate(
            flops=10_000_000_000, bytes_accessed=8_000_000, transcendentals=0
        ),
        name="estimate_shifts",
    )(offsets, ref, sec, *halos, four, spec, lift, corr, jnp.asarray(lags)[:, None],
      jnp.asarray(lag_wide), jnp.pad(offsets, ((0, 0), (0, LANES - chips))).astype(jnp.float32))


def resample_kernel(pick_ref, rows_ref, band_ref, out_ref, wide):
    owned = out_ref.shape[1]
    piece = rows_ref.shape[1]
    count = (wide.shape[1] - 2 * MARGIN) // piece
    total = count * piece
    at = pl.program_id(0)

    @pl.when(at == 0)
    def _():
        wide[:, :MARGIN] = jnp.zeros((2 * owned, MARGIN), jnp.bfloat16)
        wide[:, MARGIN + total : 2 * MARGIN + total] = jnp.zeros((2 * owned, MARGIN), jnp.bfloat16)
        for r in range(count):
            lines = dot(pick_ref[pl.ds(r * 2 * owned, 2 * owned), :], rows_ref[...])
            wide[:, MARGIN + r * piece : MARGIN + (r + 1) * piece] = lines.astype(jnp.bfloat16)

    first = at * piece
    for k in range(piece // LANES):
        window = wide[:, pl.ds(pl.multiple_of(first + k * LANES, LANES), 2 * LANES)]
        s = dot(window, band_ref[k])
        out_ref[0, :, k * LANES : (k + 1) * LANES] = s[:owned]
        out_ref[1, :, k * LANES : (k + 1) * LANES] = s[owned:]


def resample(pick, rows, bands, owner_cap):
    piece = rows.shape[1]
    blocks = piece // LANES
    count = bands.shape[0] // blocks
    return pl.pallas_call(
        resample_kernel,
        grid=(count,),
        in_specs=[
            pl.BlockSpec(pick.shape, lambda i: (0, 0)),
            pl.BlockSpec(rows.shape, lambda i: (0, 0)),
            pl.BlockSpec((blocks, 2 * LANES, LANES), lambda i: (i, 0, 0)),
        ],
        out_specs=pl.BlockSpec((2, owner_cap, piece), lambda i: (0, 0, i)),
        out_shape=jax.ShapeDtypeStruct((2, owner_cap, count * piece), jnp.float32),
        scratch_shapes=[pltpu.VMEM((2 * owner_cap, count * piece + 2 * MARGIN), jnp.bfloat16)],
        compiler_params=pltpu.CompilerParams(vmem_limit_bytes=VMEM_LIMIT),
        cost_estimate=pl.CostEstimate(
            flops=6_000_000_000, bytes_accessed=12_000_000, transcendentals=0
        ),
        name="resample",
    )(pick, rows, bands)


def rotate_kernel(tile_ref, est_ref, lines_ref, out_ref, turns):
    owned = out_ref.shape[1]
    count = pl.num_programs(0)
    at = pl.program_id(0)
    tiles = est_ref.shape[0] // count
    tile = tile_ref[...]

    @pl.when(at == 0)
    def _():
        angle = PHASE_RATE * est_ref[...]
        turns[0] = jnp.cos(angle)
        turns[1] = jnp.sin(angle)

    cosine = jnp.zeros((owned, LANES), jnp.float32)
    sine = jnp.zeros((owned, LANES), jnp.float32)
    for a in range(tiles):
        cosine = jnp.where(tile == a, turns[0, pl.ds(a * count + at, 1), :], cosine)
        sine = jnp.where(tile == a, turns[1, pl.ds(a * count + at, 1), :], sine)
    lane = lax.broadcasted_iota(jnp.int32, (owned, LANES), 1) // SPACING
    for k in range(out_ref.shape[2] // LANES):
        chip = lane + k * (LANES // SPACING)
        cos_k = jnp.take_along_axis(cosine, chip, axis=1)
        sin_k = jnp.take_along_axis(sine, chip, axis=1)
        cols = slice(k * LANES, (k + 1) * LANES)
        s_re = lines_ref[0, :, cols]
        s_im = lines_ref[1, :, cols]
        out_ref[0, :, cols] = (s_re * cos_k + s_im * sin_k).astype(jnp.bfloat16)
        out_ref[1, :, cols] = (s_im * cos_k - s_re * sin_k).astype(jnp.bfloat16)


def rotate(tile, est, lines, count):
    piece = lines.shape[2] // count
    return pl.pallas_call(
        rotate_kernel,
        grid=(count,),
        in_specs=[
            pl.BlockSpec(tile.shape, lambda i: (0, 0)),
            pl.BlockSpec(est.shape, lambda i: (0, 0)),
            pl.BlockSpec((2, lines.shape[1], piece), lambda i: (0, 0, i)),
        ],
        out_specs=pl.BlockSpec((2, lines.shape[1], piece), lambda i: (0, 0, i)),
        out_shape=jax.ShapeDtypeStruct(lines.shape, jnp.bfloat16),
        scratch_shapes=[pltpu.VMEM((2,) + est.shape, jnp.float32)],
        name="rotate",
    )(tile, est, lines)


def per_device(
    reference_slc, secondary_slc, chip_offsets, src_row, line_owner, band_start, band_taps
):
    tables = make_tables()
    lines_dev = secondary_slc.shape[1]
    cols_dev = secondary_slc.shape[2]
    chip_count = cols_dev // SPACING
    az_count = lax.axis_size("az")
    rg_count = lax.axis_size("rg")
    owners = az_count * rg_count
    pair_cap = max(2, (lines_dev + 2 * MAX_SHIFT + owners - 1) // owners)
    owner_cap = pair_cap * az_count
    total_cols = cols_dev * rg_count
    first_row = lines_dev // 2 - CHIP_LEN // 2
    az_index = lax.axis_index("az")
    rg_index = lax.axis_index("rg")
    me_owner = az_index * rg_count + rg_index

    low_rows = secondary_slc[:, lines_dev - MARGIN :, :]
    top_rows = secondary_slc[:, :MARGIN, :]
    last = cols_dev - MARGIN
    edges = jnp.concatenate(
        [secondary_slc, reference_slc[:, first_row : first_row + CHIP_LEN, :]], axis=1
    )
    sends = (
        (low_rows, 1, 0),
        (top_rows, -1, 0),
        (edges[:, :, last:], 0, 1),
        (edges[:, :, :MARGIN], 0, -1),
        (low_rows[:, :, last:], 1, 1),
        (low_rows[:, :, :MARGIN], 1, -1),
        (top_rows[:, :, last:], -1, 1),
        (top_rows[:, :, :MARGIN], -1, -1),
    )
    halos = []
    for which, send in enumerate(sends):
        halos.append(moved(*send))

    count = src_row.shape[0]
    ids = jnp.arange(count, dtype=jnp.int32)
    src_tile = src_row // lines_dev
    mine = (line_owner[:, None] == line_owner[None, :]) & (ids[:, None] < ids[None, :])
    own_rank = jnp.sum(mine.astype(jnp.int32), axis=0)
    near = mine & (src_tile[:, None] == src_tile[None, :])
    pair_rank = jnp.sum(near.astype(jnp.int32), axis=0)

    local_row = src_row - az_index * lines_dev
    slot = jnp.where(src_tile == az_index, line_owner * pair_cap + pair_rank, -1)
    slots = jnp.arange(owners * pair_cap, dtype=jnp.int32)
    send_row = jnp.sum(
        jnp.where(slots[:, None] == slot[None, :], local_row[None, :] + 1, 0), axis=1
    ) - 1
    send_row = send_row.reshape(owners, 1, pair_cap)
    part = jnp.arange(2, dtype=jnp.int32)[None, :, None] * lines_dev
    target = jnp.where(send_row >= 0, send_row + part, -1).reshape(-1)
    send_pick = (
        target[:, None] == jnp.arange(2 * lines_dev, dtype=jnp.int32)[None, :]
    ).astype(jnp.bfloat16)
    outgoing = gather_rows(send_pick, secondary_slc)
    arrived = lax.all_to_all(
        outgoing, ("az", "rg"), split_axis=0, concat_axis=0, tiled=True
    )

    offsets = chip_offsets[:, 0]
    est, spread = estimate_shifts(
        offsets, reference_slc, secondary_slc, halos, tables, owners
    )
    est = est[:, :chip_count]
    everywhere = lax.all_to_all(
        spread,
        ("az", "rg"),
        split_axis=0,
        concat_axis=0,
        tiled=True,
    )

    all_cols = jnp.arange(total_cols, dtype=jnp.int32)
    rel = (band_start - all_cols // LANES * LANES + MARGIN)[None, :]
    bands = build_bands(rel, band_taps)

    outs = jnp.arange(owner_cap, dtype=jnp.int32)
    placed = (own_rank[None, :] == outs[:, None]) & (line_owner == me_owner)[None, :]
    which = jnp.sum(
        jnp.where(placed, (src_tile * pair_cap + pair_rank + 1)[None, :], 0), axis=1
    ) - 1
    tile = which // pair_cap
    from_rank = which % pair_cap
    rg_ids = jnp.arange(rg_count, dtype=jnp.int32)[:, None, None]
    parts = jnp.arange(2, dtype=jnp.int32)[None, :, None]
    source = ((tile[None, None] * rg_count + rg_ids) * 2 + parts) * pair_cap + from_rank[None, None]
    source = jnp.where(which[None, None] >= 0, source, -1).reshape(-1)
    recv_pick = (
        source[:, None] == jnp.arange(owners * 2 * pair_cap, dtype=jnp.int32)[None, :]
    ).astype(jnp.bfloat16)

    lines = resample(recv_pick, arrived, bands, owner_cap)
    tile_wide = jnp.broadcast_to(tile[:, None], (owner_cap, LANES))
    lines_out = rotate(tile_wide, everywhere, lines, rg_count)
    return (est[:, None, :], lines_out)


def solution(mesh):
    return jax.shard_map(
        per_device,
        mesh=mesh,
        in_specs=(
            P(None, "az", "rg"),
            P(None, "az", "rg"),
            P(None, "az", "rg"),
            P(),
            P(),
            P(),
            P(),
        ),
        out_specs=(P(None, "az", "rg"), P(None, ("az", "rg"), None)),
        check_vma=False,
    )
```
